32 devices in a mesh: cuts: 4 (over y, core), mesh: 8 (over z, x).
Axes of the slice: x: 2, y: 2, z: 4, core: 2. Of those that a mesh axis runs over, the one named last changes fastest.
Arguments:
- start_modes: float32 [128, 16384], P('cuts', 'mesh'), may hold values from -6 to 6
- connectivity: int32 [125, 256], P(None, 'mesh'), may hold values from 0 to 2047, as said below
- stiffness_weights: float32 [125, 256], P(None, 'mesh'), may hold values from 0.5 to 4
- shared_nodes: int32 [2, 4096], P(None, 'mesh'), may hold values from 0 to 2047, as said below
- node_mass: float32 [16384], P('mesh'), may hold values from 0.5 to 54
- centers: float32 [4], P('cuts'), may hold values from 20 to 200
- half_widths: float32 [4], P('cuts'), may hold values from 100 to 400
- keep_flags: int32 [4, 8], P('cuts'), may hold values 0 or 1
Outputs:
- filtered: float32 [128, 16384], P('cuts', 'mesh')
- edge_products: float32 [4, 8, 8], P('cuts')
- first_level: float32 [128, 16384], P('cuts', 'mesh')
The draws below stay inside these ranges and needn't reach their ends.
Inputs may be any that keep to these rules, and one draw needn't show every extreme that they name: `connectivity`: within each partition: entry k = 25 a + 5 b + c names the element's GLL node (a, b, c); every node index of the partition is named by some element, and neighbouring elements name the same nodes on their common faces. `shared_nodes`: within each partition the 1024 entries are distinct; entry k of row 1 of partition p and entry k of row 0 of partition p + 1 are copies of the same node.
All inputs are finite; a program needn't handle non-finite values. No bound on the sum of `keep_flags` on one device may be relied on, other than what follows from the above.
Results may differ from the reference program's by a relative error of at most 0.0001.
Values sent between devices are 32-bit elements; how exact they have to be, the bound alone decides.
A program may use at most 64 MiB of HBM per device.

```python
import math
import jax
import jax.numpy as jnp
import numpy as np
from jax import lax

MODES = 32
EDGE = 8
ELEM_DEV = 32
SHARED = 512
NODES_DEV = 2048
ELEMS = 256
NODES = 16384
N_CUTS = 4
N_MESH = 8


def node_labels(key):
    partitions = NODES // NODES_DEV

    def one_part(part_index):
        inner = jax.random.permutation(jax.random.fold_in(jax.random.fold_in(key, 71), part_index), NODES_DEV - 2) + 1
        return jnp.concatenate([jnp.zeros((1,), jnp.int32), inner.astype(jnp.int32), jnp.full((1,), NODES_DEV - 1, jnp.int32)])
    return jax.vmap(one_part)(jnp.arange(partitions))


def draw_connectivity(key, part):
    labels = node_labels(key)
    partitions = NODES // NODES_DEV
    span_x = NODES_DEV // 512
    element = jnp.arange(ELEM_DEV)
    elem_z = element % 8
    elem_y = element // 8 % 4
    elem_x = element // 32
    entry = jnp.arange(125)
    node_a = entry // 25
    node_b = entry // 5 % 5
    node_c = entry % 5
    pos_x = (4 * elem_x[None, :] + node_a[:, None]) % span_x
    pos_y = (4 * elem_y[None, :] + node_b[:, None]) % 16
    pos_z = (4 * elem_z[None, :] + node_c[:, None]) % 32
    lattice = (pos_x * 16 + pos_y) * 32 + pos_z
    per_part = jnp.take(labels, lattice, axis=1)

    def shuffle(part_index, columns):
        column_order = jax.random.permutation(jax.random.fold_in(jax.random.fold_in(key, 83), part_index), ELEM_DEV)
        return jnp.take(columns, column_order.astype(jnp.int32), axis=1)
    per_part = jax.vmap(shuffle)(jnp.arange(partitions), per_part)
    return per_part.transpose(1, 0, 2).reshape(125, ELEM_DEV * partitions).astype(jnp.int32)


def draw_shared_nodes(key, part):
    labels = node_labels(key)
    partitions = NODES // NODES_DEV

    def pairing(part_index):
        return jax.random.permutation(jax.random.fold_in(jax.random.fold_in(key, 89), part_index), SHARED).astype(jnp.int32)
    pairings = jax.vmap(pairing)(jnp.arange(partitions))
    shifted_pairs = jnp.roll(pairings, 1, axis=0)
    lower = jnp.take_along_axis(labels[:, :SHARED], shifted_pairs, axis=1)
    upper = jnp.take_along_axis(labels[:, NODES_DEV - SHARED:], pairings, axis=1)
    return jnp.stack([lower, upper]).reshape(2, partitions * SHARED).astype(jnp.int32)


def draw_node_mass(key, part):
    partitions = NODES // NODES_DEV
    rising = (jnp.arange(NODES) // NODES_DEV).astype(jnp.float32) / (partitions - 1)
    base = jnp.exp(jax.random.uniform(key, (NODES,), jnp.float32, math.log(0.5), math.log(5.0)))
    return base * 3.0 ** rising


def with_ends(drawn, rng, smallest, largest):
    dims = drawn.shape
    index_at = [jax.random.randint(jax.random.fold_in(rng, axis), (), 0, dims[axis]) for axis in range(len(dims))]
    drawn = drawn.at[tuple(index_at)].set(smallest)
    longest = dims.index(max(dims))
    index_at[longest] = (index_at[longest] + 1) % dims[longest]
    return drawn.at[tuple(index_at)].set(largest)


def steps_of(rng, dims, cuts, low, high):
    factor_of = 1.0
    for dim, blocks in cuts:
        steps = jax.random.uniform(jax.random.fold_in(jax.random.fold_in(rng, 6), dim), (blocks,), jnp.float32, low / len(cuts), high / len(cuts))
        factor_of = factor_of * jnp.repeat(jnp.exp(steps), dims[dim] // blocks).reshape((-1,) + (1,) * (len(dims) - 1 - dim))
    return factor_of


def centred(stream_key, shape, spread, most, cuts=(), kind=jnp.bfloat16):
    loudness = steps_of(stream_key, shape, cuts, -0.22, 0.18) if cuts else 1.0
    values = jax.random.normal(stream_key, shape, jnp.float32) * spread * loudness
    return jnp.minimum(jnp.maximum(values, -most), most).astype(kind)


def setup_inputs(seed: int = 0) -> dict:
    arg_keys = jax.random.split(jax.random.key(seed), 9)
    start_modes = centred(arg_keys[0], (N_CUTS * MODES, NODES), 1.0, 6.0, ((0, 4), (1, 8)), jnp.float32)
    connectivity = draw_connectivity(jax.random.fold_in(arg_keys[8], 71), 0)
    stiffness_weights = jnp.clip(jnp.exp(math.log(4.0) - 2.0794415 * jax.random.uniform(arg_keys[2], (125, ELEMS), jnp.float32) ** steps_of(arg_keys[2], (125, ELEMS), ((1, 8),), -0.2, 0.2)), 0.5, 4.0)
    shared_nodes = draw_shared_nodes(jax.random.fold_in(arg_keys[8], 71), 0)
    node_mass = draw_node_mass(jax.random.fold_in(arg_keys[8], 71), 0)
    centers = jnp.clip(20.0 + 180.0 * jax.random.uniform(arg_keys[5], (N_CUTS,), jnp.float32) ** steps_of(arg_keys[5], (N_CUTS,), ((0, 4),), -0.2, 0.2), 20.0, 200.0)
    half_widths = jnp.clip(jnp.exp(math.log(400.0) - 1.3862944 * jax.random.uniform(arg_keys[6], (N_CUTS,), jnp.float32) ** steps_of(arg_keys[6], (N_CUTS,), ((0, 4),), -0.2, 0.2)), 100.0, 400.0)
    keep_flags = with_ends((jax.random.randint(arg_keys[7], (N_CUTS, EDGE), 0, 4) < 3).astype(jnp.int32), jax.random.fold_in(arg_keys[7], 1), 0, 1)
    return {"start_modes": start_modes, "connectivity": connectivity, "stiffness_weights": stiffness_weights, "shared_nodes": shared_nodes, "node_mass": node_mass, "centers": centers, "half_widths": half_widths, "keep_flags": keep_flags}


epsilon = 1e-06
highest = lax.Precision.HIGHEST

def gll_derivative():
    points = np.array([-1.0, -math.sqrt(3.0 / 7.0), 0.0, math.sqrt(3.0 / 7.0), 1.0])
    barycentric = np.array([1.0 / np.prod([points[j] - points[k] for k in range(5) if k != j]) for j in range(5)])
    table = np.zeros((5, 5))
    for row_index in range(5):
        for col_index in range(5):
            if row_index != col_index:
                table[row_index, col_index] = barycentric[col_index] / barycentric[row_index] / (points[row_index] - points[col_index])
        table[row_index, row_index] = -np.sum(table[row_index])
    return table

def stiffness(fields, conn_part, weight_part, derivative):
    row_count = fields.shape[0]
    elements = conn_part.shape[1]
    values = jnp.take(fields, conn_part, axis=1).reshape(row_count, 5, 5, 5, elements)
    weight = weight_part.reshape(5, 5, 5, elements)
    grad_a = jnp.einsum('ia,mabce->mibce', derivative, values, precision=highest)
    grad_b = jnp.einsum('jb,mabce->majce', derivative, values, precision=highest)
    grad_c = jnp.einsum('kc,mabce->mabke', derivative, values, precision=highest)
    returned = jnp.einsum('ia,mibce->mabce', derivative, weight * grad_a, precision=highest)
    returned = returned + jnp.einsum('jb,majce->mabce', derivative, weight * grad_b, precision=highest)
    returned = returned + jnp.einsum('kc,mabke->mabce', derivative, weight * grad_c, precision=highest)
    returned = returned.reshape(row_count, 125, elements)
    return jnp.zeros(fields.shape, fields.dtype).at[:, conn_part].add(returned)

def operate(fields, connectivity, stiffness_weights, shared_nodes, node_mass, derivative):
    row_count = fields.shape[0]
    per_part = fields.reshape(row_count, N_MESH, NODES_DEV).transpose(1, 0, 2)
    conn_parts = connectivity.reshape(125, N_MESH, ELEM_DEV).transpose(1, 0, 2)
    weight_parts = stiffness_weights.reshape(125, N_MESH, ELEM_DEV).transpose(1, 0, 2)
    applied = lax.map(lambda bundle: stiffness(bundle[0], bundle[1], bundle[2], derivative), (per_part, conn_parts, weight_parts))
    shared_parts = shared_nodes.reshape(2, N_MESH, SHARED).transpose(1, 0, 2)
    lower_vals = jax.vmap(lambda values_part, index_part: values_part[:, index_part])(applied, shared_parts[:, 0])
    upper_vals = jax.vmap(lambda values_part, index_part: values_part[:, index_part])(applied, shared_parts[:, 1])
    padding = jnp.zeros((1, row_count, SHARED), applied.dtype)
    from_below = jnp.concatenate([padding, upper_vals[:-1]], axis=0)
    from_above = jnp.concatenate([lower_vals[1:], padding], axis=0)
    adder = jax.vmap(lambda values_part, index_part, extra: values_part.at[:, index_part].add(extra))
    applied = adder(applied, shared_parts[:, 0], from_below)
    applied = adder(applied, shared_parts[:, 1], from_above)
    return applied.transpose(1, 0, 2).reshape(row_count, NODES) / node_mass

def reference(start_modes, connectivity, stiffness_weights, shared_nodes, node_mass, centers, half_widths, keep_flags):
    derivative = jnp.asarray(gll_derivative(), jnp.float32)
    filtered_list = []
    level_list = []
    for cut_index in range(N_CUTS):
        start = start_modes[cut_index * MODES:(cut_index + 1) * MODES]
        center = centers[cut_index]
        half_width = half_widths[cut_index]
        first_step = (operate(start, connectivity, stiffness_weights, shared_nodes, node_mass, derivative) - center * start) / half_width
        first_norms = lax.optimization_barrier(jnp.sum(node_mass * first_step * first_step, axis=1))
        first_scale = lax.rsqrt(first_norms / NODES + epsilon)
        level_one = first_step * first_scale[:, None]
        level_zero = start * first_scale[:, None]
        applied = operate(level_one, connectivity, stiffness_weights, shared_nodes, node_mass, derivative)
        second_step = 2.0 * (applied - center * level_one) / half_width - level_zero
        second_norms = lax.optimization_barrier(jnp.sum(node_mass * second_step * second_step, axis=1))
        filtered_list.append(second_step * lax.rsqrt(second_norms / NODES + epsilon)[:, None])
        level_list.append(level_one)
    products = [jnp.zeros((EDGE, EDGE), jnp.float32)]
    for cut_index in range(1, N_CUTS):
        upper_rows = filtered_list[cut_index - 1][MODES - EDGE:] * node_mass
        lower_rows = filtered_list[cut_index][:EDGE]
        inner = jnp.einsum('in,jn->ij', upper_rows, lower_rows, precision=highest)
        products.append(inner * keep_flags[cut_index].astype(jnp.float32)[None, :] / math.sqrt(NODES))
    return (jnp.concatenate(filtered_list, axis=0), jnp.stack(products), jnp.concatenate(level_list, axis=0))
```

```python
import functools
import math

import jax
import jax.numpy as jnp
import numpy as np
from jax import lax
from jax.experimental import pallas as pl
from jax.experimental.pallas import tpu as pltpu
from jax.sharding import PartitionSpec as P

epsilon = 1e-06
LOW = 256
MESH = pl.DeviceIdType.MESH
bf16 = jnp.bfloat16
f32 = jnp.float32


def gll_derivative():
    points = np.array([-1.0, -math.sqrt(3.0 / 7.0), 0.0, math.sqrt(3.0 / 7.0), 1.0])
    barycentric = np.array(
        [1.0 / np.prod([points[j] - points[k] for k in range(5) if k != j]) for j in range(5)]
    )
    table = np.zeros((5, 5))
    for row_index in range(5):
        for col_index in range(5):
            if row_index != col_index:
                table[row_index, col_index] = (
                    barycentric[col_index]
                    / barycentric[row_index]
                    / (points[row_index] - points[col_index])
                )
        table[row_index, row_index] = -np.sum(table[row_index])
    return table


def apply5(table, u):
    even = [u[0] + u[4], u[1] + u[3]]
    odd = [u[0] - u[4], u[1] - u[3]]
    out = [None] * 5
    for i in range(2):
        s = [float((table[i, j] + table[i, 4 - j]) / 2) for j in range(2)]
        t = [float((table[i, j] - table[i, 4 - j]) / 2) for j in range(2)]
        p = s[0] * even[0] + s[1] * even[1] + float(table[i, 2]) * u[2]
        q = t[0] * odd[0] + t[1] * odd[1]
        out[i] = q + p
        out[4 - i] = q - p
    t = [float((table[2, j] - table[2, 4 - j]) / 2) for j in range(2)]
    out[2] = t[0] * odd[0] + t[1] * odd[1]
    return out


def transpose4(x):
    lane = lax.broadcasted_iota(jnp.int32, x[0].shape, 1)
    left = lane < 64
    even = (lane % 64) < 32
    y = [None] * 4
    for g in range(2):
        a, b = x[g], x[g + 2]
        y[g] = jnp.where(left, a, pltpu.roll(b, 64, 1))
        y[g + 2] = jnp.where(left, pltpu.roll(a, 64, 1), b)
    z = [None] * 4
    for g in (0, 2):
        a, b = y[g], y[g + 1]
        z[g] = jnp.where(even, a, pltpu.roll(b, 32, 1))
        z[g + 1] = jnp.where(even, pltpu.roll(a, 96, 1), b)
    return z


def split2(x):
    high = x.astype(bf16)
    low = (x - high.astype(f32)).astype(bf16)
    return high, low


def kernel(
    n_mesh,
    n_cuts,
    total_nodes,
    v_ref,
    conn_ref,
    w_ref,
    shared_ref,
    mass_ref,
    center_ref,
    half_ref,
    keep_ref,
    filt_ref,
    edge_ref,
    level_ref,
    conn_s,
    onehot,
    mask_f,
    mask_b,
    sh_onehot,
    sh_mask_f,
    sh_mask_b,
    w_s,
    u_s,
    r_s,
    src_s,
    scat_s,
    sh_scat_s,
    first_s,
    second_s,
    tx,
    rx,
    edge_tx,
    edge_rx,
    block,
    blocks,
    halo_send,
    halo_recv,
    edge_send,
    edge_recv,
    sum_send,
    sum_recv,
):
    me = lax.axis_index("mesh")
    cut = lax.axis_index("cuts")
    modes, nodes = v_ref.shape
    groups = modes // 8
    highs = nodes // LOW
    local, elements = conn_ref.shape
    shared = shared_ref.shape[1]
    edge_count = keep_ref.shape[1]
    table = gll_derivative()

    barrier = pltpu.get_barrier_semaphore()

    def greet(d, carry):
        pl.semaphore_signal(
            barrier,
            inc=1,
            device_id={"mesh": lax.rem(me + d, n_mesh)},
            device_id_type=MESH,
        )
        return carry

    lax.fori_loop(1, n_mesh, greet, 0)

    @pl.when(cut > 0)
    def _():
        pl.semaphore_signal(
            barrier, inc=1, device_id={"cuts": cut - 1}, device_id_type=MESH
        )

    @pl.when(cut < n_cuts - 1)
    def _():
        pl.semaphore_signal(
            barrier, inc=1, device_id={"cuts": cut + 1}, device_id_type=MESH
        )

    conn_s[...] = jnp.full(conn_s.shape, -1, jnp.int32)
    conn_s[0:local, :] = conn_ref[...]
    chunks = conn_s.shape[0] // 4
    index = jnp.concatenate(
        [conn_s[pl.ds(q, chunks, stride=4), :] for q in range(4)], axis=1
    )
    row_low = lax.broadcasted_iota(jnp.int32, (LOW, 128), 0)
    row_high = lax.broadcasted_iota(jnp.int32, (highs, 128), 0)

    def tables(row, cols, hot, mf, mb):
        low = row & (LOW - 1)
        high = row >> 8
        one = (row_low == low).astype(f32).astype(bf16)
        hot[0:LOW, cols] = one
        hot[LOW:, cols] = one
        m = (row_high == high).astype(f32)
        mf[:, cols] = m
        for h in range(highs):
            mb[h, :, cols] = jnp.broadcast_to(m[h : h + 1], (16, 128)).astype(bf16)

    for r in range(chunks):
        tables(index[r : r + 1], slice(r * 128, r * 128 + 128), onehot, mask_f, mask_b)
    per_row = shared // 128
    for r in range(2 * per_row):
        row = shared_ref[r // per_row : r // per_row + 1, r % per_row * 128 : r % per_row * 128 + 128]
        tables(row, slice(r * 128, r * 128 + 128), sh_onehot, sh_mask_f, sh_mask_b)
    w4 = jnp.concatenate([w_ref[...]] * 4, axis=1)
    for k in range(local):
        w_s[k] = jnp.broadcast_to(w4[k : k + 1], (8, 128))
    r_s[local:] = jnp.zeros((r_s.shape[0] - local, 8, 128), f32)

    inv_mass = 1.0 / mass_ref[...]
    center = center_ref[0]
    inv_half = 1.0 / jnp.full((1, 128), half_ref[0], f32)[:, 0:1]

    def load_source(x):
        high, low = split2(x)
        for h in range(highs):
            src_s[h * modes : (h + 1) * modes, 0:LOW] = high[:, h * LOW : (h + 1) * LOW]
            src_s[h * modes : (h + 1) * modes, LOW:] = low[:, h * LOW : (h + 1) * LOW]

    def gather(hot, mf, cols):
        res = jnp.dot(src_s[...], hot[:, cols], preferred_element_type=f32)
        out = res[0:modes] * mf[0:1, cols]
        for h in range(1, highs):
            out = out + res[h * modes : (h + 1) * modes] * mf[h : h + 1, cols]
        return out

    def place(x, dst, mb, cols):
        high, low = split2(x)
        both = jnp.concatenate([high, low], axis=0)
        for h in range(highs):
            m = mb[h, :, cols]
            for i in range(2 * modes // 16):
                dst[h * 2 * modes + i * 16 : h * 2 * modes + i * 16 + 16, cols] = (
                    both[i * 16 : i * 16 + 16] * m
                )

    def scatter(dst, hot):
        res = lax.dot_general(
            dst[...],
            hot[0:LOW, :],
            (((1,), (1,)), ((), ())),
            preferred_element_type=f32,
        )
        return jnp.concatenate(
            [
                res[h * 2 * modes : h * 2 * modes + modes]
                + res[h * 2 * modes + modes : (h + 1) * 2 * modes]
                for h in range(highs)
            ],
            axis=1,
        )

    def axis_pass(base_of, stride, first):
        def line(l, carry):
            base = base_of(l)
            u = [u_s[base + i * stride] for i in range(5)]
            g = apply5(table, u)
            g = [g[i] * w_s[base + i * stride] for i in range(5)]
            back = apply5(table.T, g)
            for i in range(5):
                k = base + i * stride
                r_s[k] = back[i] if first else r_s[k] + back[i]
            return carry

        lax.fori_loop(0, 25, line, 0, unroll=5)

    def halo(step):
        up = pltpu.make_async_remote_copy(
            src_ref=tx.at[step, 1],
            dst_ref=rx.at[step, 0],
            send_sem=halo_send.at[step, 0],
            recv_sem=halo_recv.at[step, 0],
            device_id={"mesh": lax.rem(me + 1, n_mesh)},
            device_id_type=MESH,
        )
        down = pltpu.make_async_remote_copy(
            src_ref=tx.at[step, 0],
            dst_ref=rx.at[step, 1],
            send_sem=halo_send.at[step, 1],
            recv_sem=halo_recv.at[step, 1],
            device_id={"mesh": lax.rem(me + n_mesh - 1, n_mesh)},
            device_id_type=MESH,
        )
        return up, down

    @pl.when(me == 0)
    def _():
        for step in range(2):
            rx[step, 0] = jnp.zeros((modes, shared), f32)

    @pl.when(me == n_mesh - 1)
    def _():
        for step in range(2):
            rx[step, 1] = jnp.zeros((modes, shared), f32)

    @pl.when(cut == 0)
    def _():
        edge_rx[...] = jnp.zeros(edge_rx.shape, f32)

    def operate(x, step):
        load_source(x)
        for t in range(chunks // 2):
            out = gather(onehot, mask_f, slice(t * 256, t * 256 + 256))
            for half in range(2):
                r = 2 * t + half
                piece = [
                    out[g * 8 : g * 8 + 8, half * 128 : half * 128 + 128] for g in range(4)
                ]
                for q, y in enumerate(transpose4(piece)):
                    u_s[4 * r + q] = y
        axis_pass(lambda l: 5 * l, 1, True)
        axis_pass(lambda l: 25 * (l // 5) + l % 5, 5, False)
        axis_pass(lambda l: l, 25, False)
        for r in range(chunks):
            piece = transpose4([r_s[4 * r + q] for q in range(4)])
            place(
                jnp.concatenate(piece, axis=0), scat_s, mask_b, slice(r * 128, r * 128 + 128)
            )
        applied = scatter(scat_s, onehot)
        load_source(applied)
        for t in range(2 * shared // 256):
            out = gather(sh_onehot, sh_mask_f, slice(t * 256, t * 256 + 256))
            at = t * 256
            tx[step, at // shared, :, at % shared : at % shared + 256] = out
        if step == 0:
            pl.semaphore_wait(
                barrier,
                n_mesh - 1 + jnp.minimum(cut, 1) + jnp.minimum(n_cuts - 1 - cut, 1),
            )
        up, down = halo(step)

        @pl.when(me < n_mesh - 1)
        def _():
            up.start()

        @pl.when(me > 0)
        def _():
            down.start()

        @pl.when(me > 0)
        def _():
            up.wait_recv()

        @pl.when(me < n_mesh - 1)
        def _():
            down.wait_recv()

        for side in range(2):
            for j in range(per_row):
                x_in = rx[step, side, :, j * 128 : j * 128 + 128]
                at = (side * per_row + j) * 128
                place(x_in, sh_scat_s, sh_mask_b, slice(at, at + 128))
        return (applied + scatter(sh_scat_s, sh_onehot)) * inv_mass

    start = v_ref[...]
    first_s[...] = (operate(start, 0) - center * start) * inv_half
    first = first_s[...]
    mass = mass_ref[...]
    first_sum = jnp.sum(mass * first * first, axis=1, keepdims=True)
    second_s[...] = 2.0 * (operate(first, 1) - center * first_s[...]) * inv_half - v_ref[...]

    edge_tx[:, 0:nodes] = second_s[modes - edge_count :, :]
    edge_tx[:, nodes:] = jnp.broadcast_to(first_sum[modes - edge_count :], (edge_count, 128))
    edge_copy = pltpu.make_async_remote_copy(
        src_ref=edge_tx,
        dst_ref=edge_rx,
        send_sem=edge_send,
        recv_sem=edge_recv,
        device_id={"cuts": lax.rem(cut + 1, n_cuts)},
        device_id_type=MESH,
    )

    @pl.when(cut < n_cuts - 1)
    def _():
        edge_copy.start()

    second = second_s[...]
    second_sum = jnp.sum(mass * second * second, axis=1, keepdims=True)

    def columns(a, b):
        lane = lax.broadcasted_iota(jnp.int32, (a.shape[0], 128), 1)
        return jnp.where(lane == 0, a, jnp.where(lane == 1, b, 0.0))

    block[0:modes, :] = columns(first_sum, second_sum)
    block[modes + edge_count :, :] = jnp.zeros((edge_count, 128), f32)

    @pl.when(cut > 0)
    def _():
        edge_copy.wait_recv()

    received = edge_rx[:, 0:nodes]
    weighted = received * mass
    block[modes : modes + edge_count, :] = columns(
        edge_rx[:, nodes:][:, 0:1], jnp.sum(weighted * received, axis=1, keepdims=True)
    )
    inner = lax.dot_general(
        weighted,
        second,
        (((1,), (1,)), ((), ())),
        preferred_element_type=f32,
        precision=lax.Precision.HIGHEST,
    )
    block[modes + edge_count :, 0:modes] = inner

    def sum_copy(d):
        return pltpu.make_async_remote_copy(
            src_ref=block,
            dst_ref=blocks.at[me],
            send_sem=sum_send.at[d],
            recv_sem=sum_recv.at[d],
            device_id={"mesh": lax.rem(me + d, n_mesh)},
            device_id_type=MESH,
        )

    def start_sum(d, carry):
        sum_copy(d).start()
        return carry

    lax.fori_loop(1, n_mesh, start_sum, 0)
    blocks[me] = block[...]

    def wait_sum(d, carry):
        sum_copy(d).wait_recv()
        return carry

    lax.fori_loop(1, n_mesh, wait_sum, 0)
    total = lax.fori_loop(1, n_mesh, lambda i, acc: acc + blocks[i], blocks[0])

    scale = lax.rsqrt(total[:, 0:1] / total_nodes + epsilon)
    own = scale * lax.rsqrt(scale * scale * total[:, 1:2] / total_nodes + epsilon)
    level_ref[...] = first_s[...] * scale[0:modes]
    filt_ref[...] = second_s[...] * own[0:modes]
    eye = lax.broadcasted_iota(jnp.int32, (modes, modes), 0) == lax.broadcasted_iota(
        jnp.int32, (modes, modes), 1
    )
    own_row = jnp.sum(
        jnp.where(eye, jnp.broadcast_to(own[0:modes], (modes, modes)), 0.0),
        axis=0,
        keepdims=True,
    )
    products = (
        total[modes + edge_count :, 0:edge_count]
        * own[modes : modes + edge_count]
        * own_row[:, 0:edge_count]
        * keep_ref[...].astype(f32)
        * (1.0 / math.sqrt(total_nodes))
    )
    edge_ref[...] = products

    for step in range(2):
        up, down = halo(step)

        @pl.when(me < n_mesh - 1)
        def _():
            up.wait_send()

        @pl.when(me > 0)
        def _():
            down.wait_send()

    @pl.when(cut < n_cuts - 1)
    def _():
        edge_copy.wait_send()

    def wait_sent(d, carry):
        sum_copy(d).wait_send()
        return carry

    lax.fori_loop(1, n_mesh, wait_sent, 0)


def per_device(
    start_modes,
    connectivity,
    stiffness_weights,
    shared_nodes,
    node_mass,
    centers,
    half_widths,
    keep_flags,
):
    n_mesh = lax.axis_size("mesh")
    n_cuts = lax.axis_size("cuts")
    modes, nodes = start_modes.shape
    local, elements = connectivity.shape
    shared = shared_nodes.shape[1]
    edge_count = keep_flags.shape[1]
    highs = nodes // LOW
    padded = -(-local // 8) * 8
    entries = padded * elements
    vmem = pl.BlockSpec(memory_space=pltpu.VMEM)
    smem = pl.BlockSpec(memory_space=pltpu.SMEM)
    dma = pltpu.SemaphoreType.DMA
    filtered, products, level = pl.pallas_call(
        functools.partial(kernel, n_mesh, n_cuts, nodes * n_mesh),
        out_shape=(
            jax.ShapeDtypeStruct((modes, nodes), f32),
            jax.ShapeDtypeStruct((edge_count, edge_count), f32),
            jax.ShapeDtypeStruct((modes, nodes), f32),
        ),
        in_specs=[vmem, vmem, vmem, vmem, vmem, smem, smem, vmem],
        out_specs=(vmem, vmem, vmem),
        scratch_shapes=[
            pltpu.VMEM((padded, elements), jnp.int32),
            pltpu.VMEM((2 * LOW, entries), bf16),
            pltpu.VMEM((highs, entries), f32),
            pltpu.VMEM((highs, 16, entries), bf16),
            pltpu.VMEM((2 * LOW, 2 * shared), bf16),
            pltpu.VMEM((highs, 2 * shared), f32),
            pltpu.VMEM((highs, 16, 2 * shared), bf16),
            pltpu.VMEM((padded, 8, 128), f32),
            pltpu.VMEM((padded, 8, 128), f32),
            pltpu.VMEM((padded, 8, 128), f32),
            pltpu.VMEM((highs * modes, 2 * LOW), bf16),
            pltpu.VMEM((highs * 2 * modes, entries), bf16),
            pltpu.VMEM((highs * 2 * modes, 2 * shared), bf16),
            pltpu.VMEM((modes, nodes), f32),
            pltpu.VMEM((modes, nodes), f32),
            pltpu.VMEM((2, 2, modes, shared), f32),
            pltpu.VMEM((2, 2, modes, shared), f32),
            pltpu.VMEM((edge_count, nodes + 128), f32),
            pltpu.VMEM((edge_count, nodes + 128), f32),
            pltpu.VMEM((modes + 2 * edge_count, 128), f32),
            pltpu.VMEM((n_mesh, modes + 2 * edge_count, 128), f32),
            dma((2, 2)),
            dma((2, 2)),
            dma,
            dma,
            dma((n_mesh,)),
            dma((n_mesh,)),
        ],
        compiler_params=pltpu.CompilerParams(collective_id=0, has_side_effects=True),
    )(
        start_modes,
        connectivity,
        stiffness_weights,
        shared_nodes,
        node_mass.reshape(1, nodes),
        centers,
        half_widths,
        keep_flags,
    )
    return filtered, products[None], level


def solution(mesh):
    return jax.shard_map(
        per_device,
        mesh=mesh,
        in_specs=(
            P("cuts", "mesh"),
            P(None, "mesh"),
            P(None, "mesh"),
            P(None, "mesh"),
            P("mesh"),
            P("cuts"),
            P("cuts"),
            P("cuts", None),
        ),
        out_specs=(P("cuts", "mesh"), P("cuts", None, None), P("cuts", "mesh")),
        check_vma=False,
    )
```

```python
import functools
import math

import jax
import jax.numpy as jnp
import numpy as np
from jax import lax
from jax.experimental import pallas as pl
from jax.experimental.pallas import tpu as pltpu
from jax.sharding import PartitionSpec as P

epsilon = 1e-06
LOW = 256
MESH = pl.DeviceIdType.MESH
bf16 = jnp.bfloat16
f32 = jnp.float32


def gll_derivative():
    points = np.array([-1.0, -math.sqrt(3.0 / 7.0), 0.0, math.sqrt(3.0 / 7.0), 1.0])
    barycentric = np.array(
        [1.0 / np.prod([points[j] - points[k] for k in range(5) if k != j]) for j in range(5)]
    )
    table = np.zeros((5, 5))
    for row_index in range(5):
        for col_index in range(5):
            if row_index != col_index:
                table[row_index, col_index] = (
                    barycentric[col_index]
                    / barycentric[row_index]
                    / (points[row_index] - points[col_index])
                )
        table[row_index, row_index] = -np.sum(table[row_index])
    return table


def apply5(table, u):
    even = [u[0] + u[4], u[1] + u[3]]
    odd = [u[0] - u[4], u[1] - u[3]]
    out = [None] * 5
    for i in range(2):
        s = [float((table[i, j] + table[i, 4 - j]) / 2) for j in range(2)]
        t = [float((table[i, j] - table[i, 4 - j]) / 2) for j in range(2)]
        p = s[0] * even[0] + s[1] * even[1] + float(table[i, 2]) * u[2]
        q = t[0] * odd[0] + t[1] * odd[1]
        out[i] = q + p
        out[4 - i] = q - p
    t = [float((table[2, j] - table[2, 4 - j]) / 2) for j in range(2)]
    out[2] = t[0] * odd[0] + t[1] * odd[1]
    return out


def transpose4(x):
    lane = lax.broadcasted_iota(jnp.int32, x[0].shape, 1)
    left = lane < 64
    even = (lane % 64) < 32
    y = [None] * 4
    for g in range(2):
        a, b = x[g], x[g + 2]
        y[g] = jnp.where(left, a, pltpu.roll(b, 64, 1))
        y[g + 2] = jnp.where(left, pltpu.roll(a, 64, 1), b)
    z = [None] * 4
    for g in (0, 2):
        a, b = y[g], y[g + 1]
        z[g] = jnp.where(even, a, pltpu.roll(b, 32, 1))
        z[g + 1] = jnp.where(even, pltpu.roll(a, 96, 1), b)
    return z


def split2(x):
    high = x.astype(bf16)
    low = (x - high.astype(f32)).astype(bf16)
    return high, low


def kernel(
    n_mesh,
    n_cuts,
    total_nodes,
    v_ref,
    conn_ref,
    w_ref,
    shared_ref,
    mass_ref,
    center_ref,
    half_ref,
    first_s,
    second_s,
    total_ref,
    turn_s,
    conn_s,
    onehot,
    mask_f,
    mask_b,
    sh_onehot,
    sh_mask_f,
    sh_mask_b,
    w_s,
    u_s,
    r_s,
    src_s,
    scat_s,
    sh_scat_s,
    tx,
    rx,
    edge_tx,
    edge_rx,
    block,
    blocks,
    halo_send,
    halo_recv,
    edge_send,
    edge_recv,
    sum_send,
    sum_recv,
):
    me = lax.axis_index("mesh")
    cut = lax.axis_index("cuts")
    modes, nodes = v_ref.shape
    groups = modes // 8
    highs = nodes // LOW
    elements, local = conn_ref.shape
    shared = shared_ref.shape[1]
    edge_count = edge_tx.shape[0]
    table = gll_derivative()

    barrier = pltpu.get_barrier_semaphore()

    def greet(d, carry):
        pl.semaphore_signal(
            barrier,
            inc=1,
            device_id={"mesh": lax.rem(me + d, n_mesh)},
            device_id_type=MESH,
        )
        return carry

    lax.fori_loop(1, n_mesh, greet, 0)

    @pl.when(cut > 0)
    def _():
        pl.semaphore_signal(
            barrier, inc=1, device_id={"cuts": cut - 1}, device_id_type=MESH
        )

    @pl.when(cut < n_cuts - 1)
    def _():
        pl.semaphore_signal(
            barrier, inc=1, device_id={"cuts": cut + 1}, device_id_type=MESH
        )

    turn_s[...] = jnp.full(turn_s.shape, -1.0, f32)
    turn_s[0:elements, 0:local] = conn_ref[...].astype(f32)
    turn_s[elements : 2 * elements, 0:local] = w_ref[...]
    turned = turn_s[...].T
    conn_s[...] = turned[:, 0:elements].astype(jnp.int32)
    chunks = conn_s.shape[0] // 4
    index = jnp.concatenate(
        [conn_s[pl.ds(q, chunks, stride=4), :] for q in range(4)], axis=1
    )
    row_low = lax.broadcasted_iota(jnp.int32, (LOW, 128), 0)
    row_high = lax.broadcasted_iota(jnp.int32, (highs, 128), 0)

    def tables(row, cols, hot, mf, mb):
        low = row & (LOW - 1)
        high = row >> 8
        one = (row_low == low).astype(f32).astype(bf16)
        hot[0:LOW, cols] = one
        hot[LOW:, cols] = one
        m = (row_high == high).astype(f32)
        mf[:, cols] = m
        for h in range(highs if mb is not None else 0):
            mb[h, :, cols] = jnp.broadcast_to(m[h : h + 1], (16, 128)).astype(bf16)

    for r in range(chunks):
        tables(index[r : r + 1], slice(r * 128, r * 128 + 128), onehot, mask_f, mask_b)
    per_row = shared // 128
    for r in range(2 * per_row):
        row = shared_ref[r // per_row : r // per_row + 1, r % per_row * 128 : r % per_row * 128 + 128]
        tables(row, slice(r * 128, r * 128 + 128), sh_onehot, sh_mask_f, None)
    w4 = jnp.concatenate([turned[:, elements : 2 * elements]] * 4, axis=1)
    for k in range(local):
        w_s[k] = jnp.broadcast_to(w4[k : k + 1], (8, 128))
    r_s[local:] = jnp.zeros((r_s.shape[0] - local, 8, 128), f32)

    inv_mass = 1.0 / mass_ref[...]
    center = center_ref[0]
    inv_half = 1.0 / jnp.full((1, 128), half_ref[0], f32)[:, 0:1]

    def load_source(x):
        high, low = split2(x)
        for h in range(highs):
            src_s[h * modes : (h + 1) * modes, 0:LOW] = high[:, h * LOW : (h + 1) * LOW]
            src_s[h * modes : (h + 1) * modes, LOW:] = low[:, h * LOW : (h + 1) * LOW]

    def gather(hot, mf, cols):
        res = jnp.dot(src_s[...], hot[:, cols], preferred_element_type=f32)
        out = res[0:modes] * mf[0:1, cols]
        for h in range(1, highs):
            out = out + res[h * modes : (h + 1) * modes] * mf[h : h + 1, cols]
        return out

    def place(x, dst, mb, cols):
        high, low = split2(x)
        both = jnp.concatenate([high, low], axis=0)
        for h in range(highs):
            m = mb[h, :, cols]
            for i in range(2 * modes // 16):
                dst[h * 2 * modes + i * 16 : h * 2 * modes + i * 16 + 16, cols] = (
                    both[i * 16 : i * 16 + 16] * m
                )

    def scatter(dst, hot):
        res = lax.dot_general(
            dst[...],
            hot[0:LOW, :],
            (((1,), (1,)), ((), ())),
            preferred_element_type=f32,
        )
        return jnp.concatenate(
            [
                res[h * 2 * modes : h * 2 * modes + modes]
                + res[h * 2 * modes + modes : (h + 1) * 2 * modes]
                for h in range(highs)
            ],
            axis=1,
        )

    def axis_pass(base_of, stride, first):
        def line(l, carry):
            base = base_of(l)
            u = [u_s[base + i * stride] for i in range(5)]
            g = apply5(table, u)
            g = [g[i] * w_s[base + i * stride] for i in range(5)]
            back = apply5(table.T, g)
            for i in range(5):
                k = base + i * stride
                r_s[k] = back[i] if first else r_s[k] + back[i]
            return carry

        lax.fori_loop(0, 25, line, 0, unroll=5)

    def halo(step):
        up = pltpu.make_async_remote_copy(
            src_ref=tx.at[step, 1],
            dst_ref=rx.at[step, 0],
            send_sem=halo_send.at[step, 0],
            recv_sem=halo_recv.at[step, 0],
            device_id={"mesh": lax.rem(me + 1, n_mesh)},
            device_id_type=MESH,
        )
        down = pltpu.make_async_remote_copy(
            src_ref=tx.at[step, 0],
            dst_ref=rx.at[step, 1],
            send_sem=halo_send.at[step, 1],
            recv_sem=halo_recv.at[step, 1],
            device_id={"mesh": lax.rem(me + n_mesh - 1, n_mesh)},
            device_id_type=MESH,
        )
        return up, down

    @pl.when(me == 0)
    def _():
        for step in range(2):
            rx[step, 0] = jnp.zeros((modes, shared), f32)

    @pl.when(me == n_mesh - 1)
    def _():
        for step in range(2):
            rx[step, 1] = jnp.zeros((modes, shared), f32)

    @pl.when(cut == 0)
    def _():
        edge_rx[...] = jnp.zeros(edge_rx.shape, f32)

    def operate(x, step, between):
        load_source(x)
        for t in range(chunks // 2):
            out = gather(onehot, mask_f, slice(t * 256, t * 256 + 256))
            for half in range(2):
                r = 2 * t + half
                piece = [
                    out[g * 8 : g * 8 + 8, half * 128 : half * 128 + 128] for g in range(4)
                ]
                for q, y in enumerate(transpose4(piece)):
                    u_s[4 * r + q] = y
        axis_pass(lambda l: 5 * l, 1, True)
        axis_pass(lambda l: 25 * (l // 5) + l % 5, 5, False)
        axis_pass(lambda l: l, 25, False)
        for r in range(chunks):
            piece = transpose4([r_s[4 * r + q] for q in range(4)])
            place(
                jnp.concatenate(piece, axis=0), scat_s, mask_b, slice(r * 128, r * 128 + 128)
            )
        applied = scatter(scat_s, onehot)
        load_source(applied)
        up, down = halo(step)
        for t in range(2 * shared // 256):
            out = gather(sh_onehot, sh_mask_f, slice(t * 256, t * 256 + 256))
            at = t * 256
            tx[step, at // shared, :, at % shared : at % shared + 256] = out
            if at + 256 == shared:
                if step == 0:
                    pl.semaphore_wait(
                        barrier,
                        n_mesh - 1 + jnp.minimum(cut, 1) + jnp.minimum(n_cuts - 1 - cut, 1),
                    )

                @pl.when(me > 0)
                def _():
                    down.start()

        @pl.when(me < n_mesh - 1)
        def _():
            up.start()

        between()

        @pl.when(me > 0)
        def _():
            up.wait_recv()

        @pl.when(me < n_mesh - 1)
        def _():
            down.wait_recv()

        for side in range(2):
            for j in range(per_row):
                x_in = rx[step, side, :, j * 128 : j * 128 + 128]
                at = (side * per_row + j) * 128
                place(x_in, sh_scat_s, sh_mask_b, slice(at, at + 128))
        return (applied + scatter(sh_scat_s, sh_onehot)) * inv_mass

    start = v_ref[...]
    mass = mass_ref[...]
    turn_s[...] = jnp.zeros(turn_s.shape, f32)

    def masks():
        for r in range(2 * per_row):
            cols = slice(r * 128, r * 128 + 128)
            for h in range(highs):
                sh_mask_b[h, :, cols] = jnp.broadcast_to(
                    sh_mask_f[h : h + 1, cols], (16, 128)
                ).astype(bf16)

    def first_column():
        level = first_s[...]
        lane = lax.broadcasted_iota(jnp.int32, (modes, 128), 1)
        turn_s[0:modes, :] = jnp.where(
            lane == 0, jnp.sum(mass * level * level, axis=1, keepdims=True), 0.0
        )

    first_s[...] = (operate(start, 0, masks) - center * start) * inv_half
    first = first_s[...]
    second_s[...] = 2.0 * (operate(first, 1, first_column) - center * first_s[...]) * inv_half - v_ref[...]

    first_sum = turn_s[0:modes, 0:1]
    edge_tx[:, 0:nodes] = second_s[modes - edge_count :, :]
    edge_tx[:, nodes:] = jnp.broadcast_to(first_sum[modes - edge_count :], (edge_count, 128))
    edge_copy = pltpu.make_async_remote_copy(
        src_ref=edge_tx,
        dst_ref=edge_rx,
        send_sem=edge_send,
        recv_sem=edge_recv,
        device_id={"cuts": lax.rem(cut + 1, n_cuts)},
        device_id_type=MESH,
    )

    @pl.when(cut < n_cuts - 1)
    def _():
        edge_copy.start()

    second = second_s[...]
    second_sum = jnp.sum(mass * second * second, axis=1, keepdims=True)

    def columns(a, b):
        lane = lax.broadcasted_iota(jnp.int32, (a.shape[0], 128), 1)
        return jnp.where(lane == 0, a, jnp.where(lane == 1, b, 0.0))

    turn_s[0:modes, :] = columns(first_sum, second_sum)

    @pl.when(cut > 0)
    def _():
        edge_copy.wait_recv()

    received = edge_rx[:, 0:nodes]
    weighted = received * mass
    turn_s[modes : modes + edge_count, :] = columns(
        edge_rx[:, nodes:][:, 0:1], jnp.sum(weighted * received, axis=1, keepdims=True)
    )
    inner = lax.dot_general(
        weighted,
        second,
        (((1,), (1,)), ((), ())),
        preferred_element_type=f32,
        precision=lax.Precision.HIGHEST,
    )
    turn_s[modes + edge_count : modes + 2 * edge_count, 0:modes] = inner
    block[...] = turn_s[...].T[0:8]

    def sum_copy(d):
        return pltpu.make_async_remote_copy(
            src_ref=block,
            dst_ref=blocks.at[me],
            send_sem=sum_send.at[d],
            recv_sem=sum_recv.at[d],
            device_id={"mesh": lax.rem(me + d, n_mesh)},
            device_id_type=MESH,
        )

    def start_sum(d, carry):
        sum_copy(d).start()
        return carry

    lax.fori_loop(1, n_mesh, start_sum, 0)
    blocks[me] = block[...]

    def wait_sum(d, carry):
        sum_copy(d).wait_recv()
        return carry

    lax.fori_loop(1, n_mesh, wait_sum, 0)
    total = lax.fori_loop(1, n_mesh, lambda i, acc: acc + blocks[i], blocks[0])

    total_ref[...] = total

    for step in range(2):
        up, down = halo(step)

        @pl.when(me < n_mesh - 1)
        def _():
            up.wait_send()

        @pl.when(me > 0)
        def _():
            down.wait_send()

    @pl.when(cut < n_cuts - 1)
    def _():
        edge_copy.wait_send()

    def wait_sent(d, carry):
        sum_copy(d).wait_send()
        return carry

    lax.fori_loop(1, n_mesh, wait_sent, 0)


def finish(total_nodes, first_ref, second_ref, total_ref, keep_ref, filt_ref, edge_ref, level_ref):
    modes = first_ref.shape[0]
    edge_count = keep_ref.shape[1]
    total = jnp.concatenate([total_ref[...], jnp.zeros((120, 128), f32)], axis=0).T
    scale = lax.rsqrt(total[:, 0:1] / total_nodes + epsilon)
    own = scale * lax.rsqrt(scale * scale * total[:, 1:2] / total_nodes + epsilon)
    level_ref[...] = first_ref[...] * scale[0:modes]
    filt_ref[...] = second_ref[...] * own[0:modes]
    eye = lax.broadcasted_iota(jnp.int32, (modes, modes), 0) == lax.broadcasted_iota(
        jnp.int32, (modes, modes), 1
    )
    own_row = jnp.sum(
        jnp.where(eye, jnp.broadcast_to(own[0:modes], (modes, modes)), 0.0),
        axis=0,
        keepdims=True,
    )
    products = (
        total[modes + edge_count : modes + 2 * edge_count, 0:edge_count]
        * own[modes : modes + edge_count]
        * own_row[:, 0:edge_count]
        * keep_ref[...].astype(f32)
        * (1.0 / math.sqrt(total_nodes))
    )
    edge_ref[0] = products


def per_device(
    start_modes,
    connectivity,
    stiffness_weights,
    shared_nodes,
    node_mass,
    centers,
    half_widths,
    keep_flags,
):
    n_mesh = lax.axis_size("mesh")
    n_cuts = lax.axis_size("cuts")
    modes, nodes = start_modes.shape
    local, elements = connectivity.shape
    shared = shared_nodes.shape[1]
    edge_count = keep_flags.shape[1]
    highs = nodes // LOW
    padded = -(-local // 8) * 8
    entries = padded * elements
    vmem = pl.BlockSpec(memory_space=pltpu.VMEM)
    smem = pl.BlockSpec(memory_space=pltpu.SMEM)
    dma = pltpu.SemaphoreType.DMA
    first, second, total = pl.pallas_call(
        functools.partial(kernel, n_mesh, n_cuts, nodes * n_mesh),
        out_shape=(
            jax.ShapeDtypeStruct((modes, nodes), f32),
            jax.ShapeDtypeStruct((modes, nodes), f32),
            jax.ShapeDtypeStruct((8, 128), f32),
        ),
        in_specs=[vmem, vmem, vmem, vmem, vmem, smem, smem],
        out_specs=(vmem, vmem, vmem),
        scratch_shapes=[
            pltpu.VMEM((128, 128), f32),
            pltpu.VMEM((padded, elements), jnp.int32),
            pltpu.VMEM((2 * LOW, entries), bf16),
            pltpu.VMEM((highs, entries), f32),
            pltpu.VMEM((highs, 16, entries), bf16),
            pltpu.VMEM((2 * LOW, 2 * shared), bf16),
            pltpu.VMEM((highs, 2 * shared), f32),
            pltpu.VMEM((highs, 16, 2 * shared), bf16),
            pltpu.VMEM((padded, 8, 128), f32),
            pltpu.VMEM((padded, 8, 128), f32),
            pltpu.VMEM((padded, 8, 128), f32),
            pltpu.VMEM((highs * modes, 2 * LOW), bf16),
            pltpu.VMEM((highs * 2 * modes, entries), bf16),
            pltpu.VMEM((highs * 2 * modes, 2 * shared), bf16),
            pltpu.VMEM((2, 2, modes, shared), f32),
            pltpu.VMEM((2, 2, modes, shared), f32),
            pltpu.VMEM((edge_count, nodes + 128), f32),
            pltpu.VMEM((edge_count, nodes + 128), f32),
            pltpu.VMEM((8, 128), f32),
            pltpu.VMEM((n_mesh, 8, 128), f32),
            dma((2, 2)),
            dma((2, 2)),
            dma,
            dma,
            dma((n_mesh,)),
            dma((n_mesh,)),
        ],
        compiler_params=pltpu.CompilerParams(collective_id=0, has_side_effects=True),
    )(
        start_modes,
        connectivity.T,
        stiffness_weights.T,
        shared_nodes,
        node_mass.reshape(1, nodes),
        centers,
        half_widths,
    )
    return pl.pallas_call(
        functools.partial(finish, nodes * n_mesh),
        out_shape=(
            jax.ShapeDtypeStruct((modes, nodes), f32),
            jax.ShapeDtypeStruct((1, edge_count, edge_count), f32),
            jax.ShapeDtypeStruct((modes, nodes), f32),
        ),
        in_specs=[vmem, vmem, vmem, vmem],
        out_specs=(vmem, vmem, vmem),
    )(first, second, total, keep_flags)


def solution(mesh):
    return jax.shard_map(
        per_device,
        mesh=mesh,
        in_specs=(
            P("cuts", "mesh"),
            P(None, "mesh"),
            P(None, "mesh"),
            P(None, "mesh"),
            P("mesh"),
            P("cuts"),
            P("cuts"),
            P("cuts", None),
        ),
        out_specs=(P("cuts", "mesh"), P("cuts", None, None), P("cuts", "mesh")),
        check_vma=False,
    )
```

```python
import functools
import math

import jax
import jax.numpy as jnp
import numpy as np
from jax import lax
from jax.experimental import pallas as pl
from jax.experimental.pallas import tpu as pltpu
from jax.sharding import PartitionSpec as P

epsilon = 1e-06
LOW = 256
MESH = pl.DeviceIdType.MESH
bf16 = jnp.bfloat16
f32 = jnp.float32


def gll_derivative():
    points = np.array([-1.0, -math.sqrt(3.0 / 7.0), 0.0, math.sqrt(3.0 / 7.0), 1.0])
    barycentric = np.array(
        [1.0 / np.prod([points[j] - points[k] for k in range(5) if k != j]) for j in range(5)]
    )
    table = np.zeros((5, 5))
    for row_index in range(5):
        for col_index in range(5):
            if row_index != col_index:
                table[row_index, col_index] = (
                    barycentric[col_index]
                    / barycentric[row_index]
                    / (points[row_index] - points[col_index])
                )
        table[row_index, row_index] = -np.sum(table[row_index])
    return table


def apply5(table, u):
    even = [u[0] + u[4], u[1] + u[3]]
    odd = [u[0] - u[4], u[1] - u[3]]
    out = [None] * 5
    for i in range(2):
        s = [float((table[i, j] + table[i, 4 - j]) / 2) for j in range(2)]
        t = [float((table[i, j] - table[i, 4 - j]) / 2) for j in range(2)]
        p = s[0] * even[0] + s[1] * even[1] + float(table[i, 2]) * u[2]
        q = t[0] * odd[0] + t[1] * odd[1]
        out[i] = q + p
        out[4 - i] = q - p
    t = [float((table[2, j] - table[2, 4 - j]) / 2) for j in range(2)]
    out[2] = t[0] * odd[0] + t[1] * odd[1]
    return out


def transpose4(x):
    lane = lax.broadcasted_iota(jnp.int32, x[0].shape, 1)
    left = lane < 64
    even = (lane % 64) < 32
    y = [None] * 4
    for g in range(2):
        a, b = x[g], x[g + 2]
        y[g] = jnp.where(left, a, pltpu.roll(b, 64, 1))
        y[g + 2] = jnp.where(left, pltpu.roll(a, 64, 1), b)
    z = [None] * 4
    for g in (0, 2):
        a, b = y[g], y[g + 1]
        z[g] = jnp.where(even, a, pltpu.roll(b, 32, 1))
        z[g + 1] = jnp.where(even, pltpu.roll(a, 96, 1), b)
    return z


def split2(x):
    high = x.astype(bf16)
    low = (x - high.astype(f32)).astype(bf16)
    return high, low


def kernel(
    n_mesh,
    n_cuts,
    total_nodes,
    v_ref,
    conn_ref,
    w_ref,
    shared_ref,
    mass_ref,
    center_ref,
    half_ref,
    first_s,
    second_s,
    total_ref,
    turn_s,
    conn_s,
    onehot,
    mask_f,
    mask_b,
    sh_onehot,
    sh_mask_f,
    sh_mask_b,
    w_s,
    u_s,
    r_s,
    src_s,
    scat_s,
    sh_scat_s,
    tx,
    rx,
    edge_tx,
    edge_rx,
    block,
    blocks,
    halo_send,
    halo_recv,
    edge_send,
    edge_recv,
    sum_send,
    sum_recv,
):
    me = lax.axis_index("mesh")
    cut = lax.axis_index("cuts")
    modes, nodes = v_ref.shape
    groups = modes // 8
    highs = nodes // LOW
    elements, local = conn_ref.shape
    shared = shared_ref.shape[1]
    edge_count = edge_tx.shape[0]
    table = gll_derivative()

    barrier = pltpu.get_barrier_semaphore()

    def greet(d, carry):
        pl.semaphore_signal(
            barrier,
            inc=1,
            device_id={"mesh": lax.rem(me + d, n_mesh)},
            device_id_type=MESH,
        )
        return carry

    lax.fori_loop(1, n_mesh, greet, 0)

    @pl.when(cut > 0)
    def _():
        pl.semaphore_signal(
            barrier, inc=1, device_id={"cuts": cut - 1}, device_id_type=MESH
        )

    @pl.when(cut < n_cuts - 1)
    def _():
        pl.semaphore_signal(
            barrier, inc=1, device_id={"cuts": cut + 1}, device_id_type=MESH
        )

    turn_s[...] = jnp.full(turn_s.shape, -1.0, f32)
    turn_s[0:elements, 0:local] = conn_ref[...].astype(f32)
    turn_s[elements : 2 * elements, 0:local] = w_ref[...]
    turned = turn_s[...].T
    conn_s[...] = turned[:, 0:elements].astype(jnp.int32)
    chunks = conn_s.shape[0] // 4
    index = jnp.concatenate(
        [conn_s[pl.ds(q, chunks, stride=4), :] for q in range(4)], axis=1
    )
    row_low = lax.broadcasted_iota(jnp.int32, (LOW, 128), 0)
    row_high = lax.broadcasted_iota(jnp.int32, (highs, 128), 0)

    def tables(row, cols, hot, mf, mb):
        low = row & (LOW - 1)
        high = row >> 8
        one = (row_low == low).astype(f32).astype(bf16)
        hot[0:LOW, cols] = one
        hot[LOW:, cols] = one
        m = (row_high == high).astype(f32)
        mf[:, cols] = m
        for h in range(highs if mb is not None else 0):
            mb[h, :, cols] = jnp.broadcast_to(m[h : h + 1], (16, 128)).astype(bf16)

    for r in range(chunks):
        tables(index[r : r + 1], slice(r * 128, r * 128 + 128), onehot, mask_f, mask_b)
    per_row = shared // 128
    for r in range(2 * per_row):
        row = shared_ref[r // per_row : r // per_row + 1, r % per_row * 128 : r % per_row * 128 + 128]
        tables(row, slice(r * 128, r * 128 + 128), sh_onehot, sh_mask_f, None)
    w4 = jnp.concatenate([turned[:, elements : 2 * elements]] * 4, axis=1)
    for k in range(local):
        w_s[k] = jnp.broadcast_to(w4[k : k + 1], (8, 128))
    r_s[local:] = jnp.zeros((r_s.shape[0] - local, 8, 128), f32)

    inv_mass = 1.0 / mass_ref[...]
    center = center_ref[...]
    inv_half = 1.0 / half_ref[...]

    def load_source(x):
        high, low = split2(x)
        for h in range(highs):
            src_s[h * modes : (h + 1) * modes, 0:LOW] = high[:, h * LOW : (h + 1) * LOW]
            src_s[h * modes : (h + 1) * modes, LOW:] = low[:, h * LOW : (h + 1) * LOW]

    def gather(hot, mf, cols):
        res = jnp.dot(src_s[...], hot[:, cols], preferred_element_type=f32)
        out = res[0:modes] * mf[0:1, cols]
        for h in range(1, highs):
            out = out + res[h * modes : (h + 1) * modes] * mf[h : h + 1, cols]
        return out

    def place(x, dst, mb, cols):
        high, low = split2(x)
        both = jnp.concatenate([high, low], axis=0)
        for h in range(highs):
            m = mb[h, :, cols]
            for i in range(2 * modes // 16):
                dst[h * 2 * modes + i * 16 : h * 2 * modes + i * 16 + 16, cols] = (
                    both[i * 16 : i * 16 + 16] * m
                )

    def scatter(dst, hot):
        res = lax.dot_general(
            dst[...],
            hot[0:LOW, :],
            (((1,), (1,)), ((), ())),
            preferred_element_type=f32,
        )
        return jnp.concatenate(
            [
                res[h * 2 * modes : h * 2 * modes + modes]
                + res[h * 2 * modes + modes : (h + 1) * 2 * modes]
                for h in range(highs)
            ],
            axis=1,
        )

    def axis_pass(base_of, stride, first):
        def line(l, carry):
            base = base_of(l)
            u = [u_s[base + i * stride] for i in range(5)]
            g = apply5(table, u)
            g = [g[i] * w_s[base + i * stride] for i in range(5)]
            back = apply5(table.T, g)
            for i in range(5):
                k = base + i * stride
                r_s[k] = back[i] if first else r_s[k] + back[i]
            return carry

        lax.fori_loop(0, 25, line, 0, unroll=5)

    def halo(step):
        up = pltpu.make_async_remote_copy(
            src_ref=tx.at[step, 1],
            dst_ref=rx.at[step, 0],
            send_sem=halo_send.at[step, 0],
            recv_sem=halo_recv.at[step, 0],
            device_id={"mesh": lax.rem(me + 1, n_mesh)},
            device_id_type=MESH,
        )
        down = pltpu.make_async_remote_copy(
            src_ref=tx.at[step, 0],
            dst_ref=rx.at[step, 1],
            send_sem=halo_send.at[step, 1],
            recv_sem=halo_recv.at[step, 1],
            device_id={"mesh": lax.rem(me + n_mesh - 1, n_mesh)},
            device_id_type=MESH,
        )
        return up, down

    @pl.when(me == 0)
    def _():
        for step in range(2):
            rx[step, 0] = jnp.zeros((modes, shared), f32)

    @pl.when(me == n_mesh - 1)
    def _():
        for step in range(2):
            rx[step, 1] = jnp.zeros((modes, shared), f32)

    @pl.when(cut == 0)
    def _():
        edge_rx[...] = jnp.zeros(edge_rx.shape, f32)

    def operate(x, step, between):
        load_source(x)
        for t in range(chunks // 2):
            out = gather(onehot, mask_f, slice(t * 256, t * 256 + 256))
            for half in range(2):
                r = 2 * t + half
                piece = [
                    out[g * 8 : g * 8 + 8, half * 128 : half * 128 + 128] for g in range(4)
                ]
                for q, y in enumerate(transpose4(piece)):
                    u_s[4 * r + q] = y
        axis_pass(lambda l: 5 * l, 1, True)
        axis_pass(lambda l: 25 * (l // 5) + l % 5, 5, False)
        axis_pass(lambda l: l, 25, False)
        for r in range(chunks):
            piece = transpose4([r_s[4 * r + q] for q in range(4)])
            place(
                jnp.concatenate(piece, axis=0), scat_s, mask_b, slice(r * 128, r * 128 + 128)
            )
        applied = scatter(scat_s, onehot)
        load_source(applied)
        up, down = halo(step)
        for t in range(2 * shared // 256):
            out = gather(sh_onehot, sh_mask_f, slice(t * 256, t * 256 + 256))
            at = t * 256
            tx[step, at // shared, :, at % shared : at % shared + 256] = out
            if at + 256 == shared:
                if step == 0:
                    pl.semaphore_wait(
                        barrier,
                        n_mesh - 1 + jnp.minimum(cut, 1) + jnp.minimum(n_cuts - 1 - cut, 1),
                    )

                @pl.when(me > 0)
                def _():
                    down.start()

        @pl.when(me < n_mesh - 1)
        def _():
            up.start()

        between()

        @pl.when(me > 0)
        def _():
            up.wait_recv()

        @pl.when(me < n_mesh - 1)
        def _():
            down.wait_recv()

        for side in range(2):
            for j in range(per_row):
                x_in = rx[step, side, :, j * 128 : j * 128 + 128]
                at = (side * per_row + j) * 128
                place(x_in, sh_scat_s, sh_mask_b, slice(at, at + 128))
        return (applied + scatter(sh_scat_s, sh_onehot)) * inv_mass

    start = v_ref[...]
    mass = mass_ref[...]
    turn_s[...] = jnp.zeros(turn_s.shape, f32)

    def masks():
        for r in range(2 * per_row):
            cols = slice(r * 128, r * 128 + 128)
            for h in range(highs):
                sh_mask_b[h, :, cols] = jnp.broadcast_to(
                    sh_mask_f[h : h + 1, cols], (16, 128)
                ).astype(bf16)

    def first_column():
        level = first_s[...]
        lane = lax.broadcasted_iota(jnp.int32, (modes, 128), 1)
        turn_s[0:modes, :] = jnp.where(
            lane == 0, jnp.sum(mass * level * level, axis=1, keepdims=True), 0.0
        )

    first_s[...] = (operate(start, 0, masks) - center * start) * inv_half
    first = first_s[...]
    second_s[...] = 2.0 * (operate(first, 1, first_column) - center * first_s[...]) * inv_half - v_ref[...]

    first_sum = turn_s[0:modes, 0:1]
    edge_tx[:, 0:nodes] = second_s[modes - edge_count :, :]
    edge_tx[:, nodes:] = jnp.broadcast_to(first_sum[modes - edge_count :], (edge_count, 128))
    edge_copy = pltpu.make_async_remote_copy(
        src_ref=edge_tx,
        dst_ref=edge_rx,
        send_sem=edge_send,
        recv_sem=edge_recv,
        device_id={"cuts": lax.rem(cut + 1, n_cuts)},
        device_id_type=MESH,
    )

    @pl.when(cut < n_cuts - 1)
    def _():
        edge_copy.start()

    second = second_s[...]
    second_sum = jnp.sum(mass * second * second, axis=1, keepdims=True)

    def columns(a, b):
        lane = lax.broadcasted_iota(jnp.int32, (a.shape[0], 128), 1)
        return jnp.where(lane == 0, a, jnp.where(lane == 1, b, 0.0))

    turn_s[0:modes, :] = columns(first_sum, second_sum)

    @pl.when(cut > 0)
    def _():
        edge_copy.wait_recv()

    received = edge_rx[:, 0:nodes]
    weighted = received * mass
    turn_s[modes : modes + edge_count, :] = columns(
        edge_rx[:, nodes:][:, 0:1], jnp.sum(weighted * received, axis=1, keepdims=True)
    )
    inner = lax.dot_general(
        weighted,
        second,
        (((1,), (1,)), ((), ())),
        preferred_element_type=f32,
        precision=lax.Precision.HIGHEST,
    )
    turn_s[modes + edge_count : modes + 2 * edge_count, 0:modes] = inner
    block[...] = turn_s[...].T[0:8]

    def sum_copy(d):
        return pltpu.make_async_remote_copy(
            src_ref=block,
            dst_ref=blocks.at[me],
            send_sem=sum_send.at[d],
            recv_sem=sum_recv.at[d],
            device_id={"mesh": lax.rem(me + d, n_mesh)},
            device_id_type=MESH,
        )

    def start_sum(d, carry):
        sum_copy(d).start()
        return carry

    lax.fori_loop(1, n_mesh, start_sum, 0)
    blocks[me] = block[...]

    def wait_sum(d, carry):
        sum_copy(d).wait_recv()
        return carry

    lax.fori_loop(1, n_mesh, wait_sum, 0)
    total = lax.fori_loop(1, n_mesh, lambda i, acc: acc + blocks[i], blocks[0])

    total_ref[...] = total

    for step in range(2):
        up, down = halo(step)

        @pl.when(me < n_mesh - 1)
        def _():
            up.wait_send()

        @pl.when(me > 0)
        def _():
            down.wait_send()

    @pl.when(cut < n_cuts - 1)
    def _():
        edge_copy.wait_send()

    def wait_sent(d, carry):
        sum_copy(d).wait_send()
        return carry

    lax.fori_loop(1, n_mesh, wait_sent, 0)


def finish(total_nodes, first_ref, second_ref, total_ref, keep_ref, filt_ref, edge_ref, level_ref):
    modes = first_ref.shape[0]
    edge_count = keep_ref.shape[1]
    total = jnp.concatenate([total_ref[...], jnp.zeros((120, 128), f32)], axis=0).T
    scale = lax.rsqrt(total[:, 0:1] / total_nodes + epsilon)
    own = scale * lax.rsqrt(scale * scale * total[:, 1:2] / total_nodes + epsilon)
    level_ref[...] = first_ref[...] * scale[0:modes]
    filt_ref[...] = second_ref[...] * own[0:modes]
    eye = lax.broadcasted_iota(jnp.int32, (modes, modes), 0) == lax.broadcasted_iota(
        jnp.int32, (modes, modes), 1
    )
    own_row = jnp.sum(
        jnp.where(eye, jnp.broadcast_to(own[0:modes], (modes, modes)), 0.0),
        axis=0,
        keepdims=True,
    )
    products = (
        total[modes + edge_count : modes + 2 * edge_count, 0:edge_count]
        * own[modes : modes + edge_count]
        * own_row[:, 0:edge_count]
        * keep_ref[...].astype(f32)
        * (1.0 / math.sqrt(total_nodes))
    )
    edge_ref[0] = products


def per_device(
    start_modes,
    connectivity,
    stiffness_weights,
    shared_nodes,
    node_mass,
    centers,
    half_widths,
    keep_flags,
):
    n_mesh = lax.axis_size("mesh")
    n_cuts = lax.axis_size("cuts")
    modes, nodes = start_modes.shape
    local, elements = connectivity.shape
    shared = shared_nodes.shape[1]
    edge_count = keep_flags.shape[1]
    highs = nodes // LOW
    padded = -(-local // 8) * 8
    entries = padded * elements
    vmem = pl.BlockSpec(memory_space=pltpu.VMEM)
    dma = pltpu.SemaphoreType.DMA
    first, second, total = pl.pallas_call(
        functools.partial(kernel, n_mesh, n_cuts, nodes * n_mesh),
        out_shape=(
            jax.ShapeDtypeStruct((modes, nodes), f32),
            jax.ShapeDtypeStruct((modes, nodes), f32),
            jax.ShapeDtypeStruct((8, 128), f32),
        ),
        in_specs=[vmem, vmem, vmem, vmem, vmem, vmem, vmem],
        out_specs=(vmem, vmem, vmem),
        scratch_shapes=[
            pltpu.VMEM((128, 128), f32),
            pltpu.VMEM((padded, elements), jnp.int32),
            pltpu.VMEM((2 * LOW, entries), bf16),
            pltpu.VMEM((highs, entries), f32),
            pltpu.VMEM((highs, 16, entries), bf16),
            pltpu.VMEM((2 * LOW, 2 * shared), bf16),
            pltpu.VMEM((highs, 2 * shared), f32),
            pltpu.VMEM((highs, 16, 2 * shared), bf16),
            pltpu.VMEM((padded, 8, 128), f32),
            pltpu.VMEM((padded, 8, 128), f32),
            pltpu.VMEM((padded, 8, 128), f32),
            pltpu.VMEM((highs * modes, 2 * LOW), bf16),
            pltpu.VMEM((highs * 2 * modes, entries), bf16),
            pltpu.VMEM((highs * 2 * modes, 2 * shared), bf16),
            pltpu.VMEM((2, 2, modes, shared), f32),
            pltpu.VMEM((2, 2, modes, shared), f32),
            pltpu.VMEM((edge_count, nodes + 128), f32),
            pltpu.VMEM((edge_count, nodes + 128), f32),
            pltpu.VMEM((8, 128), f32),
            pltpu.VMEM((n_mesh, 8, 128), f32),
            dma((2, 2)),
            dma((2, 2)),
            dma,
            dma,
            dma((n_mesh,)),
            dma((n_mesh,)),
        ],
        compiler_params=pltpu.CompilerParams(collective_id=0, has_side_effects=True),
    )(
        start_modes,
        connectivity.T,
        stiffness_weights.T,
        shared_nodes,
        node_mass.reshape(1, nodes),
        centers.reshape(1, 1),
        half_widths.reshape(1, 1),
    )
    return pl.pallas_call(
        functools.partial(finish, nodes * n_mesh),
        out_shape=(
            jax.ShapeDtypeStruct((modes, nodes), f32),
            jax.ShapeDtypeStruct((1, edge_count, edge_count), f32),
            jax.ShapeDtypeStruct((modes, nodes), f32),
        ),
        in_specs=[vmem, vmem, vmem, vmem],
        out_specs=(vmem, vmem, vmem),
    )(first, second, total, keep_flags)


def solution(mesh):
    return jax.shard_map(
        per_device,
        mesh=mesh,
        in_specs=(
            P("cuts", "mesh"),
            P(None, "mesh"),
            P(None, "mesh"),
            P(None, "mesh"),
            P("mesh"),
            P("cuts"),
            P("cuts"),
            P("cuts", None),
        ),
        out_specs=(P("cuts", "mesh"), P("cuts", None, None), P("cuts", "mesh")),
        check_vma=False,
    )
```
